32 devices in a mesh: dp: 8 (over z, y), row: 2 (over x), col: 2 (over core).
Axes of the slice: x: 2, y: 2, z: 4, core: 2. Of those that a mesh axis runs over, the one named last changes fastest.
Arguments:
- hidden: bfloat16 [6144, 1024], P('dp'), may hold values from -26 to 26
- out_grad: bfloat16 [6144, 1024], P('dp', 'row'), may hold values from -4 to 4
- seq_lens: int32 [8, 4], P('dp'), may hold values from 1 to 765, as said below
- rmsnorm_gain: float32 [1024], P('row'), may hold values from 0.5 to 1.5
- w_z: bfloat16 [1024, 2048], P('row', 'col'), may hold values from -0.1875 to 0.1875
- w_x: bfloat16 [1024, 2048], P('row', 'col'), may hold values from -0.1875 to 0.1875
- w_bc: bfloat16 [1024, 256], P('row', 'col'), may hold values from -0.1875 to 0.1875
- w_dt: bfloat16 [1024, 32], P('row', 'col'), may hold values from -0.1875 to 0.1875
- conv_x: float32 [4, 2, 1024], P(None, 'col', 'row'), may hold values from -3 to 3
- conv_x_bias: float32 [2, 1024], P('col', 'row'), may hold values from -3 to 3
- conv_bc: float32 [4, 256], replicated, may hold values from -3 to 3
- conv_bc_bias: float32 [256], replicated, may hold values from -3 to 3
- dt_bias: float32 [2, 16], P('col', 'row'), may hold values from -7.5 to -4.5
- a_log: float32 [2, 16], P('col', 'row'), may hold values from 0 to 2.1
- d_skip: float32 [2, 16], P('col', 'row'), may hold values from 0.3 to 3
- gate_gain: float32 [2, 1024], P('col', 'row'), may hold values from 0.5 to 1.5
- w_out: bfloat16 [2048, 1024], P('col', 'row'), may hold values from -0.125 to 0.125
Outputs:
- block_out: bfloat16 [6144, 1024], P('dp', ('row', 'col'))
- hidden_input_gradient: bfloat16 [6144, 1024], P('dp', ('row', 'col'))
- grad_norm_gain: float32 [1024], P(('row', 'col'))
- grad_w_z: float32 [1024, 2048], P('row', 'col')
- grad_w_x: float32 [1024, 2048], P('row', 'col')
- grad_w_bc: float32 [1024, 256], P('row', 'col')
- grad_w_dt: float32 [1024, 32], P('row', 'col')
- grad_conv_x: float32 [4, 2, 1024], P(None, 'col', 'row')
- grad_conv_x_bias: float32 [2, 1024], P('col', 'row')
- grad_conv_bc: float32 [4, 256], replicated
- grad_conv_bc_bias: float32 [256], replicated
- grad_dt_bias: float32 [2, 16], P('col', 'row')
- grad_a_log: float32 [2, 16], P('col', 'row')
- grad_d_skip: float32 [2, 16], P('col', 'row')
- grad_gate_gain: float32 [2, 1024], P('col', 'row')
- grad_w_out: float32 [2048, 1024], P('col', 'row')
The draws below stay inside these ranges and needn't reach their ends.
Inputs may be any that keep to these rules, and one draw needn't show every extreme that they name: `seq_lens`: row d lists the lengths of the 4 sequences of index d of dp in the order in which they lie in its 768 token rows from row 0; each row sums to at most 768, some row to exactly 768 with one sequence of the largest length, and the rows after a row's sequences are padding.
All inputs are finite; a program needn't handle non-finite values.
Results may differ from the reference program's by a relative error of at most 0.0078.
Values may be sent and summed in bfloat16 or wider, within the bound.
A program may use at most 192 MiB of HBM per device.

```python
import math
import jax
import jax.numpy as jnp
from jax import lax

MODEL_WIDTH = 1024
E = 2048
H = 32
N = 128
K = 4
TOK_DEV = 768
SEQS = 4
TOKENS = 6144
N_DP = 8
N_COL = 2


def draw_hidden(key, part):
    base_key = jax.random.fold_in(key, 101)
    scale_key = jax.random.fold_in(key, 102)
    columns = jnp.arange(MODEL_WIDTH, dtype=jnp.float32) / (MODEL_WIDTH - 1)
    row_scale = 10.0 ** jax.random.uniform(scale_key, (TOKENS, 1), jnp.float32, -0.5, 0.5)
    values = jax.random.truncated_normal(base_key, -2.5, 2.5, (TOKENS, MODEL_WIDTH), jnp.float32)
    column_scale = 10.0 ** (columns - 0.5)
    return (values * row_scale * column_scale[None, :]).astype(jnp.bfloat16)


def draw_seq_lens(key, part):
    total_key = jax.random.fold_in(key, 201)
    share_key = jax.random.fold_in(key, 202)
    full_key = jax.random.fold_in(key, 203)
    totals = jax.random.randint(total_key, (N_DP,), TOK_DEV // 4, TOK_DEV + 1)
    chosen = jax.random.randint(full_key, (), 0, N_DP)
    totals = jnp.where(jnp.arange(N_DP) == chosen, TOK_DEV, totals).astype(jnp.int32)
    shares = jax.random.randint(share_key, (N_DP, SEQS), 1, 65)
    whole = jnp.sum(shares, axis=1, keepdims=True)
    leading = 1 + (totals[:, None] - SEQS) * shares[:, :SEQS - 1] // whole
    closing = totals - jnp.sum(leading, axis=1)
    lengths = jnp.concatenate([leading, closing[:, None]], axis=1).astype(jnp.int32)
    special = jnp.where(jnp.arange(SEQS) == 0, TOK_DEV - SEQS + 1, 1).astype(jnp.int32)
    lengths = jnp.where((jnp.arange(N_DP) == chosen)[:, None], special[None, :], lengths)
    return lengths.astype(jnp.int32)


def shard_levels(own_key, dims, split, smallest, largest):
    factor_of, own = 1.0, jax.random.fold_in(own_key, 6)
    for axis_at, shards_of in split:
        draws = jnp.exp(jax.random.uniform(jax.random.fold_in(own, axis_at), (shards_of,), jnp.float32, smallest / len(split), largest / len(split)))
        factor_of = factor_of * jnp.repeat(draws, dims[axis_at] // shards_of).reshape([-1 if axis == axis_at else 1 for axis in range(len(dims))])
    return factor_of


def gaussian(rng, shape, width, most, cuts=(), kind=jnp.bfloat16):
    drawn = jax.random.normal(rng, shape, jnp.float32) * width
    if len(cuts) > 0:
        drawn = shard_levels(rng, shape, cuts, -0.22, 0.18) * drawn
    return jnp.clip(drawn, min=-most, max=most).astype(kind)


def setup_inputs(seed: int = 0) -> dict:
    arg_keys = jax.random.split(jax.random.key(seed), 18)
    hidden = draw_hidden(jax.random.fold_in(arg_keys[17], 71), 0)
    out_grad = gaussian(arg_keys[1], (TOKENS, MODEL_WIDTH), 1.0, 4.0, ((0, 8), (1, 2)))
    seq_lens = draw_seq_lens(jax.random.fold_in(arg_keys[17], 71), 0)
    rmsnorm_gain = jnp.clip(1.0 + 0.1 * jax.random.normal(arg_keys[3], (MODEL_WIDTH,), jnp.float32), 0.5, 1.5)
    w_z = gaussian(arg_keys[4], (MODEL_WIDTH, E), MODEL_WIDTH ** -0.5, 0.1875, ((0, 2), (1, 2)))
    w_x = gaussian(arg_keys[5], (MODEL_WIDTH, E), MODEL_WIDTH ** -0.5, 0.1875, ((0, 2), (1, 2)))
    w_bc = gaussian(arg_keys[6], (MODEL_WIDTH, 2 * N), MODEL_WIDTH ** -0.5, 0.1875, ((0, 2), (1, 2)))
    w_dt = gaussian(arg_keys[7], (MODEL_WIDTH, H), MODEL_WIDTH ** -0.5, 0.1875, ((0, 2), (1, 2)))
    conv_x = gaussian(arg_keys[8], (K, N_COL, E // N_COL), 0.5, 3.0, ((1, 2), (2, 2)), jnp.float32)
    conv_x_bias = gaussian(arg_keys[9], (N_COL, E // N_COL), 0.5, 3.0, ((0, 2), (1, 2)), jnp.float32)
    conv_bc = gaussian(arg_keys[10], (K, 2 * N), 0.5, 3.0, (), jnp.float32)
    conv_bc_bias = gaussian(arg_keys[11], (2 * N,), 0.5, 3.0, (), jnp.float32)
    dt_bias = jnp.clip(-7.5 + 3.0 * jax.random.uniform(arg_keys[12], (N_COL, H // N_COL), jnp.float32) ** shard_levels(arg_keys[12], (N_COL, H // N_COL), ((0, 2), (1, 2)), -0.2, 0.2), -7.5, -4.5)
    a_log = jnp.clip(2.1 * jax.random.uniform(arg_keys[13], (N_COL, H // N_COL), jnp.float32) ** shard_levels(arg_keys[13], (N_COL, H // N_COL), ((0, 2), (1, 2)), -0.2, 0.2), 0.0, 2.1)
    d_skip = jnp.clip(jnp.exp(math.log(3.0) - 2.3025851 * jax.random.uniform(arg_keys[14], (N_COL, H // N_COL), jnp.float32) ** shard_levels(arg_keys[14], (N_COL, H // N_COL), ((0, 2), (1, 2)), -0.2, 0.2)), 0.3, 3.0)
    gate_gain = jnp.clip(1.0 + 0.1 * jax.random.normal(arg_keys[15], (N_COL, E // N_COL), jnp.float32), 0.5, 1.5)
    w_out = gaussian(arg_keys[16], (E, MODEL_WIDTH), E ** -0.5, 0.125, ((0, 2), (1, 2)))
    return {"hidden": hidden, "out_grad": out_grad, "seq_lens": seq_lens, "rmsnorm_gain": rmsnorm_gain, "w_z": w_z, "w_x": w_x, "w_bc": w_bc, "w_dt": w_dt, "conv_x": conv_x, "conv_x_bias": conv_x_bias, "conv_bc": conv_bc, "conv_bc_bias": conv_bc_bias, "dt_bias": dt_bias, "a_log": a_log, "d_skip": d_skip, "gate_gain": gate_gain, "w_out": w_out}


EPS = 1e-05
HIGHEST = lax.Precision.HIGHEST

def segments(lengths, row_count):
    ends = jnp.cumsum(lengths).astype(jnp.int32)
    places = jnp.arange(row_count, dtype=jnp.int32)
    segment = lax.optimization_barrier(jnp.sum((places[:, None] >= ends[None, :]).astype(jnp.int32), axis=1)).astype(jnp.int32)
    living = (segment < lengths.shape[0]).astype(jnp.float32)
    return (segment, living)

def depthwise(signal, weights, offset_bias, segment):
    row_count = signal.shape[0]
    total = offset_bias[None, :] + weights[0][None, :] * signal
    for offset in range(1, weights.shape[0]):
        moved = jnp.concatenate([jnp.zeros((offset, signal.shape[1]), jnp.float32), signal[:row_count - offset]], axis=0)
        earlier = jnp.concatenate([jnp.full((offset,), -1, jnp.int32), segment[:row_count - offset]])
        same_seq = (earlier == segment).astype(jnp.float32)
        total = total + weights[offset][None, :] * moved * same_seq[:, None]
    return total

def state_scan(inputs, b_rows, c_rows, steps, rates, segment, block):
    row_count, heads, head_width = inputs.shape
    width_state = b_rows.shape[1]
    count = row_count // block
    series = (inputs.reshape(count, block, heads, head_width), b_rows.reshape(count, block, width_state), c_rows.reshape(count, block, width_state), steps.reshape(count, block, heads), segment.reshape(count, block))
    places = jnp.arange(block, dtype=jnp.int32)
    causal = places[:, None] >= places[None, :]

    def advance(carry, pieces):
        state, previous = carry
        x_blk, b_blk, c_blk, step_blk, seg_blk = pieces
        logs = jnp.cumsum(-step_blk * rates[None, :], axis=0)
        same = jnp.logical_and(seg_blk[:, None] == seg_blk[None, :], causal)
        gaps = logs.T[:, :, None] - logs.T[:, None, :]
        decays = jnp.where(same[None], jnp.exp(jnp.where(same[None], gaps, 0.0)), 0.0)
        scores = jnp.dot(c_blk, b_blk.T, precision=HIGHEST)
        weighted = x_blk * step_blk[:, :, None]
        inner = jnp.einsum('hts,shp->thp', decays * scores[None], weighted, precision=HIGHEST)
        keeps = (seg_blk == previous).astype(jnp.float32)
        carried = jnp.einsum('tn,hpn->thp', c_blk, state, precision=HIGHEST)
        carried = carried * (jnp.exp(logs) * keeps[:, None])[:, :, None]
        closing = jnp.exp(logs[-1][None, :] - logs) * (seg_blk == seg_blk[-1]).astype(jnp.float32)[:, None]
        fresh = jnp.einsum('shp,sn->hpn', weighted * closing[:, :, None], b_blk, precision=HIGHEST)
        held = jnp.exp(logs[-1]) * (seg_blk[-1] == previous).astype(jnp.float32)
        state = state * held[:, None, None] + fresh
        return ((state, seg_blk[-1]), inner + carried)
    start = (jnp.zeros((heads, head_width, width_state), jnp.float32), jnp.array(-1, jnp.int32))
    final_carry, outputs = lax.scan(advance, start, series)
    return outputs.reshape(row_count, heads, head_width)

def mixer(x_part, bc_part, z_part, dt_part, conv_w, conv_b, bc_w, bc_b, dt_shift, a_logs, skips, segment, living):
    row_count = x_part.shape[0]
    heads = dt_shift.shape[0]
    x_act = jax.nn.silu(depthwise(x_part, conv_w, conv_b, segment))
    bc_act = jax.nn.silu(depthwise(bc_part, bc_w, bc_b, segment))
    width_state = bc_act.shape[1] // 2
    steps = jax.nn.softplus(dt_part + dt_shift[None, :])
    inputs = x_act.reshape(row_count, heads, -1)
    block = min(row_count, 256)
    scanned = state_scan(inputs, bc_act[:, :width_state], bc_act[:, width_state:], steps, jnp.exp(a_logs), segment, block)
    scanned = scanned + skips[None, :, None] * inputs
    return scanned.reshape(row_count, -1) * jax.nn.silu(z_part) * living[:, None]

def add_up(running, update):
    return running + update

def reference(hidden, out_grad, seq_lens, rmsnorm_gain, w_z, w_x, w_bc, w_dt, conv_x, conv_x_bias, conv_bc, conv_bc_bias, dt_bias, a_log, d_skip, gate_gain, w_out):
    conv_flat = conv_x.reshape(conv_x.shape[0], -1)
    conv_bias_flat = conv_x_bias.reshape(-1)
    shift_flat = dt_bias.reshape(-1)
    alog_flat = a_log.reshape(-1)
    skip_flat = d_skip.reshape(-1)
    gain_flat = gate_gain.reshape(-1)

    def one_block(totals, index):
        start = index * TOK_DEV
        unscaled_value = lax.dynamic_slice_in_dim(hidden, start, TOK_DEV, 0).astype(jnp.float32)
        incoming_gradient = lax.dynamic_slice_in_dim(out_grad, start, TOK_DEV, 0)
        segment, living = segments(seq_lens[index], TOK_DEV)
        inverse_root_mean = lax.rsqrt(lax.optimization_barrier(jnp.mean(unscaled_value * unscaled_value, axis=1)) + EPS)
        normalized_input = unscaled_value * inverse_root_mean[:, None]
        normalized_rows = (normalized_input * rmsnorm_gain[None, :]).astype(jnp.bfloat16)
        z_in = jnp.dot(normalized_rows, w_z, preferred_element_type=jnp.float32)
        x_in = jnp.dot(normalized_rows, w_x, preferred_element_type=jnp.float32)
        dt_in = jnp.dot(normalized_rows, w_dt, preferred_element_type=jnp.float32)
        bc_in = jnp.dot(normalized_rows, w_bc, preferred_element_type=jnp.float32)

        def local_mix(x_part, bc_part, z_part, dt_part, conv_w, conv_b, bc_w, bc_b, dt_shift, a_logs, skips):
            return mixer(x_part, bc_part, z_part, dt_part, conv_w, conv_b, bc_w, bc_b, dt_shift, a_logs, skips, segment, living)
        mixed, pull = jax.vjp(local_mix, x_in, bc_in, z_in, dt_in, conv_flat, conv_bias_flat, conv_bc, conv_bc_bias, shift_flat, alog_flat, skip_flat)
        inv_gate = lax.rsqrt(lax.optimization_barrier(jnp.mean(mixed * mixed, axis=1)) + EPS)
        gated = (mixed * inv_gate[:, None] * gain_flat[None, :]).astype(jnp.bfloat16)
        block_out = (unscaled_value + jnp.dot(gated, w_out, preferred_element_type=jnp.float32)).astype(jnp.bfloat16)
        d_gated = jnp.dot(incoming_gradient, w_out.T, preferred_element_type=jnp.float32)
        grad_w_out = jnp.dot(gated.T, incoming_gradient, preferred_element_type=jnp.float32)
        grad_gate = lax.optimization_barrier(jnp.sum(d_gated * mixed * inv_gate[:, None], axis=0))
        inner = lax.optimization_barrier(jnp.sum(mixed * gain_flat[None, :] * d_gated, axis=1))
        d_mixed = inv_gate[:, None] * gain_flat[None, :] * d_gated - mixed * (inv_gate ** 3 / E)[:, None] * inner[:, None]
        grad_x, grad_bc, grad_z, grad_dt, grad_cw, grad_cb, grad_bw, grad_bb, grad_shift, grad_alog, grad_skip = pull(d_mixed)
        z_round = grad_z.astype(jnp.bfloat16)
        x_round = grad_x.astype(jnp.bfloat16)
        dt_round = grad_dt.astype(jnp.bfloat16)
        bc_round = grad_bc.astype(jnp.bfloat16)
        normalized_gradient = jnp.dot(z_round, w_z.T, preferred_element_type=jnp.float32) + jnp.dot(x_round, w_x.T, preferred_element_type=jnp.float32) + jnp.dot(dt_round, w_dt.T, preferred_element_type=jnp.float32) + jnp.dot(bc_round, w_bc.T, preferred_element_type=jnp.float32)
        norm_gradient = lax.optimization_barrier(jnp.sum(normalized_gradient * normalized_input, axis=0))
        scaled_value = normalized_gradient * rmsnorm_gain[None, :]
        hidden_input_gradient = (incoming_gradient.astype(jnp.float32) + inverse_root_mean[:, None] * (scaled_value - normalized_input * lax.optimization_barrier(jnp.mean(scaled_value * normalized_input, axis=1))[:, None])).astype(jnp.bfloat16)
        updates = (norm_gradient, jnp.dot(normalized_rows.T, z_round, preferred_element_type=jnp.float32), jnp.dot(normalized_rows.T, x_round, preferred_element_type=jnp.float32), jnp.dot(normalized_rows.T, bc_round, preferred_element_type=jnp.float32), jnp.dot(normalized_rows.T, dt_round, preferred_element_type=jnp.float32), grad_cw, grad_cb, grad_bw, grad_bb, grad_shift, grad_alog, grad_skip, grad_gate, grad_w_out)
        totals = jax.tree.map(add_up, totals, updates)
        return (totals, (block_out, hidden_input_gradient))
    starts = (jnp.zeros((MODEL_WIDTH,), jnp.float32), jnp.zeros(w_z.shape, jnp.float32), jnp.zeros(w_x.shape, jnp.float32), jnp.zeros(w_bc.shape, jnp.float32), jnp.zeros(w_dt.shape, jnp.float32), jnp.zeros(conv_flat.shape, jnp.float32), jnp.zeros(conv_bias_flat.shape, jnp.float32), jnp.zeros(conv_bc.shape, jnp.float32), jnp.zeros(conv_bc_bias.shape, jnp.float32), jnp.zeros(shift_flat.shape, jnp.float32), jnp.zeros(alog_flat.shape, jnp.float32), jnp.zeros(skip_flat.shape, jnp.float32), jnp.zeros(gain_flat.shape, jnp.float32), jnp.zeros(w_out.shape, jnp.float32))
    totals, (outs_blocks, grads_blocks) = lax.scan(one_block, starts, jnp.arange(N_DP, dtype=jnp.int32))
    norm_gradient, grad_wz, grad_wx, grad_wbc, grad_wdt, grad_cw, grad_cb, grad_bw, grad_bb, grad_shift, grad_alog, grad_skip, grad_gate, grad_wout = totals
    return (outs_blocks.reshape(TOKENS, MODEL_WIDTH), grads_blocks.reshape(TOKENS, MODEL_WIDTH), norm_gradient, grad_wz, grad_wx, grad_wbc, grad_wdt, grad_cw.reshape(conv_x.shape), grad_cb.reshape(conv_x_bias.shape), grad_bw, grad_bb, grad_shift.reshape(dt_bias.shape), grad_alog.reshape(a_log.shape), grad_skip.reshape(d_skip.shape), grad_gate.reshape(gate_gain.shape), grad_wout)
```

```python
import functools

import jax
import jax.numpy as jnp
from jax import lax
from jax.experimental import pallas as pl
from jax.experimental.pallas import tpu as pltpu
from jax.sharding import PartitionSpec as P

EPS = 1e-05
HIGHEST = lax.Precision.HIGHEST
F32 = jnp.float32
BF16 = jnp.bfloat16
LANES = 128
NEGATIVE = -1e30


def segments(lengths, row_count):
    ends = jnp.cumsum(lengths)
    places = jnp.arange(row_count, dtype=jnp.int32)
    segment = jnp.sum((places[:, None] >= ends[None, :]).astype(jnp.int32), axis=1)
    living = (segment < lengths.shape[0]).astype(F32)
    return (segment, living)


def depthwise(signal, weights, offset_bias, segment):
    row_count = signal.shape[0]
    total = offset_bias[None, :] + weights[0][None, :] * signal
    for offset in range(1, weights.shape[0]):
        moved = jnp.concatenate(
            [jnp.zeros((offset, signal.shape[1]), F32), signal[: row_count - offset]],
            axis=0,
        )
        earlier = jnp.concatenate(
            [jnp.full((offset,), -1, jnp.int32), segment[: row_count - offset]]
        )
        same_seq = (earlier == segment).astype(F32)
        total = total + weights[offset][None, :] * moved * same_seq[:, None]
    return total


def halves(a):
    high = a.astype(BF16)
    return high, (a - high.astype(F32)).astype(BF16)


def dot3(a, b, ca=1, cb=0):
    dims = (((ca,), (cb,)), ((), ()))
    ah, al = halves(a)
    bh, bl = halves(b)

    def one(u, v):
        return lax.dot_general(u, v, dims, preferred_element_type=F32)

    return one(ah, bh) + (one(ah, bl) + one(al, bh))


def dot6(a, b):
    return jnp.dot(a, b, precision=HIGHEST, preferred_element_type=F32)


def iota(shape, axis):
    return lax.broadcasted_iota(jnp.int32, shape, axis)


def decays_of(dt, dt_t, rate_row, rate_col, heads, width):
    rows = dt.shape[0]
    lower = (iota((rows, rows), 0) >= iota((rows, rows), 1)).astype(F32)
    upper = (iota((rows, rows), 0) <= iota((rows, rows), 1)).astype(F32)
    logs = dot6(lower, -dt * rate_row)
    logs_t = dot6(-dt_t * rate_col, upper)
    spread = (iota((heads, width), 0) == iota((heads, width), 1) // (width // heads)).astype(F32)
    return logs, logs_t, upper, spread


def scan_forward(x_ref, b_ref, c_ref, dt_ref, dtt_ref, sc_ref, sr_ref, aux_ref, rr_ref, rc_ref,
                 y_ref, st_ref, state):
    @pl.when(pl.program_id(0) == 0)
    def _():
        state[...] = jnp.zeros_like(state)

    st_ref[0] = state[...]
    rows, width = x_ref.shape
    heads = dt_ref.shape[1]
    each = width // heads
    x, b, c, dt = x_ref[...], b_ref[...], c_ref[...], dt_ref[...]
    logs, logs_t, upper, spread = decays_of(dt, dtt_ref[...], rr_ref[...], rc_ref[...], heads, width)
    keep, last = aux_ref[:, 0:1], aux_ref[:, 1:2]
    grown = dot6(jnp.exp(logs), spread)
    closing = dot6(jnp.exp(logs[rows - 1 :] - logs), spread) * last
    xw = x * dot6(dt, spread)
    before = state[...]
    carried = dot3(c, before) * (grown * keep)
    mask = jnp.logical_and(sc_ref[...] == sr_ref[...], iota((rows, rows), 0) >= iota((rows, rows), 1))
    scores = dot3(c, b, 1, 1)
    per = LANES // each
    lane = iota((rows, LANES), 1) // each
    for group in range(width // LANES):
        cols = slice(group * LANES, (group + 1) * LANES)
        total = carried[:, cols]
        for j in range(per):
            h = group * per + j
            gap = logs[:, h : h + 1] - logs_t[h : h + 1, :]
            weight = jnp.exp(jnp.where(mask, gap, NEGATIVE)) * scores
            total = total + dot3(weight, jnp.where(lane == j, xw[:, cols], 0.0))
        y_ref[:, cols] = total
    held = grown[rows - 1 :] * keep[rows - 1 :]
    state[...] = before * held + dot3(b, xw * closing, 0, 0)


def scan_backward(x_ref, b_ref, c_ref, dt_ref, dtt_ref, sc_ref, sr_ref, aux_ref, rr_ref, rc_ref,
                  y_ref, st_ref, dy_ref, dx_ref, db_ref, dc_ref, ddt_ref, da_ref, dstate):
    @pl.when(pl.program_id(0) == 0)
    def _():
        dstate[...] = jnp.zeros_like(dstate)
        da_ref[...] = jnp.zeros_like(da_ref)

    rows, width = x_ref.shape
    heads = dt_ref.shape[1]
    each = width // heads
    x, b, c, dt, dy = x_ref[...], b_ref[...], c_ref[...], dt_ref[...], dy_ref[...]
    logs, logs_t, upper, spread = decays_of(dt, dtt_ref[...], rr_ref[...], rc_ref[...], heads, width)
    keep, last = aux_ref[:, 0:1], aux_ref[:, 1:2]
    grown = dot6(jnp.exp(logs), spread)
    closing = dot6(jnp.exp(logs[rows - 1 :] - logs), spread) * last
    dt_wide = dot6(dt, spread)
    xw = x * dt_wide
    before, after = st_ref[0], dstate[...]
    held = grown[rows - 1 :] * keep[rows - 1 :]
    u = dy * (grown * keep)
    dc = dot3(u, before, 1, 1)
    v = dot3(b, after)
    xc = xw * closing
    db = dot3(xc, after, 1, 1)
    tail = jnp.sum(before * after, axis=0, keepdims=True) * held + jnp.sum(v * xc, axis=0, keepdims=True)
    dstate[...] = dot3(c, u, 0, 0) + after * held
    mask = jnp.logical_and(sc_ref[...] == sr_ref[...], iota((rows, rows), 0) <= iota((rows, rows), 1))
    scores = dot3(b, c, 1, 1)
    per = LANES // each
    lane = iota((rows, LANES), 1) // each
    dscores = jnp.zeros((rows, rows), F32)
    pieces = []
    for group in range(width // LANES):
        cols = slice(group * LANES, (group + 1) * LANES)
        total = v[:, cols] * closing[:, cols]
        for j in range(per):
            h = group * per + j
            gap = logs_t[h : h + 1, :] - logs[:, h : h + 1]
            decay = jnp.exp(jnp.where(mask, gap, NEGATIVE))
            dyj = jnp.where(lane == j, dy[:, cols], 0.0)
            total = total + dot3(decay * scores, dyj)
            dscores = dscores + dot3(xw[:, cols], dyj, 1, 1) * decay
        pieces.append(total)
    dxw = jnp.concatenate(pieces, axis=1)
    db_ref[...] = db + dot3(dscores, c)
    dc_ref[...] = dc + dot3(dscores, b, 0, 0)
    gather = (iota((width, heads), 0) // each == iota((width, heads), 1)).astype(F32)
    wide = dy * y_ref[...] - xw * dxw
    wide = wide + jnp.where(iota((rows, width), 0) == rows - 1, tail, 0.0)
    dneg = dot6(upper, dot6(wide, gather))
    ddt_ref[...] = dot6(dxw * x, gather) - dneg * rr_ref[...]
    da_ref[...] = da_ref[...] - jnp.sum(dt * dneg, axis=0, keepdims=True)
    dx_ref[...] = dxw * dt_wide


def scan_specs(rows, width, state, heads, count, backward):
    def at(i):
        return count - 1 - i if backward else i

    tall = lambda n: pl.BlockSpec((rows, n), lambda i: (at(i), 0))
    flat = lambda n: pl.BlockSpec((n, rows), lambda i: (0, at(i)))
    fixed = lambda a, b: pl.BlockSpec((a, b), lambda i: (0, 0))
    ins = [tall(width), tall(state), tall(state), tall(heads), flat(heads), tall(1), flat(1),
           tall(2), fixed(1, heads), fixed(heads, 1)]
    states = pl.BlockSpec((1, state, width), lambda i: (at(i), 0, 0))
    return ins, tall, fixed, states


def scan_operands(x, b, c, dt, rates, segment, block):
    row_count = x.shape[0]
    series = segment.reshape(row_count // block, block)
    closing = series[:, -1:]
    previous = jnp.concatenate([jnp.full((1, 1), -1, jnp.int32), closing[:-1]], axis=0)
    aux = jnp.stack(
        [(series == previous).astype(F32).reshape(-1), (series == closing).astype(F32).reshape(-1)],
        axis=1,
    )
    return (x, b, c, dt, dt.T, segment[:, None], segment[None, :], aux, rates[None, :], rates[:, None])


@functools.partial(jax.custom_vjp, nondiff_argnums=(6,))
def state_scan(x, b, c, dt, rates, segment, block):
    return scan_fwd(x, b, c, dt, rates, segment, block)[0]


def scan_fwd(x, b, c, dt, rates, segment, block):
    row_count, width = x.shape
    state, heads = b.shape[1], dt.shape[1]
    count = row_count // block
    ins, tall, fixed, states = scan_specs(block, width, state, heads, count, False)
    y, kept = pl.pallas_call(
        scan_forward,
        grid=(count,),
        in_specs=ins,
        out_specs=[tall(width), states],
        out_shape=[
            jax.ShapeDtypeStruct((row_count, width), F32),
            jax.ShapeDtypeStruct((count, state, width), F32),
        ],
        scratch_shapes=[pltpu.VMEM((state, width), F32)],
        compiler_params=pltpu.CompilerParams(vmem_limit_bytes=48 * 1024 * 1024),
        cost_estimate=pl.CostEstimate(flops=2_000_000_000, bytes_accessed=6_000_000, transcendentals=0),
        name="scan_forward",
    )(*scan_operands(x, b, c, dt, rates, segment, block))
    return y, (x, b, c, dt, rates, segment, y, kept)


def scan_bwd(block, saved, dy):
    x, b, c, dt, rates, segment, y, kept = saved
    row_count, width = x.shape
    state, heads = b.shape[1], dt.shape[1]
    count = row_count // block
    ins, tall, fixed, states = scan_specs(block, width, state, heads, count, True)
    dx, db, dc, ddt, da = pl.pallas_call(
        scan_backward,
        grid=(count,),
        in_specs=ins + [tall(width), states, tall(width)],
        out_specs=[tall(width), tall(state), tall(state), tall(heads), fixed(1, heads)],
        out_shape=[
            jax.ShapeDtypeStruct((row_count, width), F32),
            jax.ShapeDtypeStruct((row_count, state), F32),
            jax.ShapeDtypeStruct((row_count, state), F32),
            jax.ShapeDtypeStruct((row_count, heads), F32),
            jax.ShapeDtypeStruct((1, heads), F32),
        ],
        scratch_shapes=[pltpu.VMEM((state, width), F32)],
        compiler_params=pltpu.CompilerParams(vmem_limit_bytes=48 * 1024 * 1024),
        cost_estimate=pl.CostEstimate(flops=6_000_000_000, bytes_accessed=10_000_000, transcendentals=0),
        name="scan_backward",
    )(*scan_operands(x, b, c, dt, rates, segment, block), y, kept, dy)
    return dx, db, dc, ddt, da[0], None


state_scan.defvjp(scan_fwd, scan_bwd)


def mixer(x_part, bc_part, z_part, dt_part, conv_w, conv_b, bc_w, bc_b, dt_shift, a_logs, skips,
          segment, living):
    row_count, width = x_part.shape
    heads = dt_shift.shape[0]
    x_act = jax.nn.silu(depthwise(x_part, conv_w, conv_b, segment))
    bc_act = jax.nn.silu(depthwise(bc_part, bc_w, bc_b, segment))
    state = bc_act.shape[1] // 2
    steps = jax.nn.softplus(dt_part + dt_shift[None, :])
    block = min(row_count, 256)
    scanned = state_scan(
        x_act, bc_act[:, :state], bc_act[:, state:], steps, jnp.exp(a_logs), segment, block
    )
    scanned = scanned + jnp.repeat(skips, width // heads)[None, :] * x_act
    return scanned * jax.nn.silu(z_part) * living[:, None]


def swap(value, axis):
    count = lax.axis_size(axis)
    return lax.ppermute(value, axis, [(i, (i + 1) % count) for i in range(count)])


def part(value, index, axis):
    size = value.shape[axis] // 2
    return lax.dynamic_slice_in_dim(value, index * size, size, axis)


def ordered(own, other, index, axis):
    first = index == 0
    return jnp.concatenate([jnp.where(first, own, other), jnp.where(first, other, own)], axis=axis)


def dot(a, b):
    return jnp.dot(a, b, preferred_element_type=F32)


def per_device(hidden, out_grad, seq_lens, rmsnorm_gain, w_z, w_x, w_bc, w_dt, conv_x, conv_x_bias,
               conv_bc, conv_bc_bias, dt_bias, a_log, d_skip, gate_gain, w_out):
    row_count, model_width = hidden.shape
    row, col = lax.axis_index("row"), lax.axis_index("col")
    batches = lax.axis_size("dp")
    shares = lax.axis_size("row") * lax.axis_size("col")
    inner_width = w_z.shape[1] * lax.axis_size("col")
    half = model_width // 2

    def own_heads(weight, axis):
        mine = part(weight, row, axis)
        theirs = swap(part(weight, 1 - row, axis), "row")
        return jnp.concatenate([mine, theirs], axis=1 - axis)

    wx = own_heads(w_x, 1)
    wbc_cols = ordered(w_bc, swap(w_bc, "col"), col, 1)
    wbc = jnp.concatenate([wbc_cols, swap(wbc_cols, "row")], axis=0)
    wdt = own_heads(w_dt, 1)
    gain = jnp.concatenate([rmsnorm_gain, swap(rmsnorm_gain, "row")])
    wz = own_heads(w_z, 1)
    incoming = jnp.concatenate([out_grad, swap(out_grad, "row")], axis=1)
    wo = own_heads(w_out, 0)

    segment, living = segments(seq_lens[0], row_count)
    whole = hidden.astype(F32)
    whole = jnp.where(row == 0, whole, jnp.concatenate([whole[:, half:], whole[:, :half]], axis=1))
    scale = lax.rsqrt(jnp.mean(whole * whole, axis=1) + EPS)
    xhat = whole * scale[:, None]
    normed = (xhat * gain[None, :]).astype(BF16)
    x_in = dot(normed, wx)
    bc_in = dot(normed, wbc)
    dt_in = dot(normed, wdt)
    z_in = dot(normed, wz)
    gain_flat = gate_gain.reshape(-1)

    def local_mix(*parts):
        return mixer(*parts, segment, living)

    mixed, pull = jax.vjp(
        local_mix, x_in, bc_in, z_in, dt_in, conv_x.reshape(conv_x.shape[0], -1),
        conv_x_bias.reshape(-1), conv_bc, conv_bc_bias, dt_bias.reshape(-1), a_log.reshape(-1),
        d_skip.reshape(-1),
    )
    d_gated = dot(incoming, wo.T)
    sums = jnp.stack(
        [jnp.sum(mixed * mixed, axis=1), jnp.sum(mixed * gain_flat[None, :] * d_gated, axis=1)]
    )
    sums = lax.psum(sums, ("row", "col"))
    inv_gate = lax.rsqrt(sums[0] / inner_width + EPS)
    inner = sums[1]
    gated = (mixed * inv_gate[:, None] * gain_flat[None, :]).astype(BF16)
    d_mixed = (
        inv_gate[:, None] * gain_flat[None, :] * d_gated
        - mixed * (inv_gate**3 / inner_width)[:, None] * inner[:, None]
    )

    def scattered(partial):
        kept = partial[:, :half] + swap(partial[:, half:].astype(BF16), "row").astype(F32)
        return part(kept, col, 1) + swap(part(kept, 1 - col, 1).astype(BF16), "col").astype(F32)

    grad_wo = dot(gated.T, incoming).astype(BF16)
    wo_piece = lax.psum_scatter(grad_wo, "dp", scatter_dimension=0, tiled=True)
    wo_pair = jnp.stack([wo_piece[:, :half], swap(wo_piece[:, half:], "row")])
    wo_pair = jnp.where(row == 0, wo_pair, wo_pair[::-1])
    wo_all = lax.all_gather(wo_pair, "dp", axis=1, tiled=True)
    grad_w_out = wo_all.reshape(-1, half).astype(F32)

    out_sum = scattered(dot(gated, wo))
    block_out = (part(whole[:, :half], col, 1) + out_sum).astype(BF16)
    grad_gate = jnp.sum(d_gated * mixed * inv_gate[:, None], axis=0)

    (grad_x, grad_bc, grad_z, grad_dt, grad_cw, grad_cb, grad_bw, grad_bb, grad_shift, grad_alog,
     grad_skip) = pull(d_mixed)
    dz, dx, ddt, dbc = (v.astype(BF16) for v in (grad_z, grad_x, grad_dt, grad_bc))

    steps = ddt.shape[1]
    grads = jnp.concatenate(
        [dz, dx, dbc, ddt, jnp.zeros((row_count, LANES - steps), BF16)], axis=1
    )
    big = dot(normed.T, grads).astype(BF16)
    wide = big.shape[1]
    big = big.reshape(2, batches, -1, wide).transpose(1, 0, 2, 3).reshape(-1, wide)
    piece = lax.psum_scatter(big, "dp", scatter_dimension=0, tiled=True)
    piece = piece.reshape(2, -1, wide)
    mine, theirs = piece[0], swap(piece[1], "row")
    nz, nbc = dz.shape[1], dbc.shape[1]
    bc_sum = (mine[:, 2 * nz : 2 * nz + nbc].astype(F32)
              + theirs[:, 2 * nz : 2 * nz + nbc].astype(F32))
    bc_sum = part(bc_sum, col, 1) + swap(part(bc_sum, 1 - col, 1).astype(BF16), "col").astype(F32)
    pieces = jnp.concatenate(
        [
            ordered(mine[:, :nz], theirs[:, :nz], row, 1),
            ordered(mine[:, nz : 2 * nz], theirs[:, nz : 2 * nz], row, 1),
            bc_sum.astype(BF16),
            jnp.where(row == 0, mine[:, 2 * nz + nbc :], theirs[:, 2 * nz + nbc :]),
            jnp.where(row == 0, theirs[:, 2 * nz + nbc :], mine[:, 2 * nz + nbc :]),
        ],
        axis=1,
    )
    whole_grads = lax.all_gather(pieces, "dp", axis=0, tiled=True)
    grad_wz = whole_grads[:, : 2 * nz].astype(F32)
    grad_wx = whole_grads[:, 2 * nz : 4 * nz].astype(F32)
    at = 4 * nz
    grad_wbc = whole_grads[:, at : at + nbc // 2].astype(F32)
    at = at + nbc // 2
    grad_wdt = jnp.concatenate(
        [whole_grads[:, at : at + steps], whole_grads[:, at + LANES : at + LANES + steps]], axis=1
    ).astype(F32)

    back = dot(dz, wz.T) + dot(dx, wx.T) + dot(ddt, wdt.T) + dot(dbc, wbc.T)
    d_normed = scattered(back)
    xhat_own = part(xhat[:, :half], col, 1)
    scaled = d_normed * part(rmsnorm_gain, col, 0)[None, :]
    total = lax.psum(jnp.sum(scaled * xhat_own, axis=1), ("row", "col"))
    hidden_input_gradient = (
        part(out_grad, col, 1).astype(F32)
        + scale[:, None] * (scaled - xhat_own * (total / model_width)[:, None])
    ).astype(BF16)
    norm_gradient = jnp.sum(d_normed * xhat_own, axis=0)

    (norm_gradient, grad_cw, grad_cb, grad_shift, grad_alog, grad_skip, grad_gate) = lax.psum(
        (norm_gradient, grad_cw, grad_cb, grad_shift, grad_alog, grad_skip, grad_gate), "dp"
    )
    grad_bw, grad_bb = lax.psum((grad_bw, grad_bb), ("dp", "row", "col"))
    return (
        block_out,
        hidden_input_gradient,
        norm_gradient,
        grad_wz,
        grad_wx,
        grad_wbc,
        grad_wdt,
        grad_cw.reshape(conv_x.shape),
        grad_cb.reshape(conv_x_bias.shape),
        grad_bw,
        grad_bb,
        grad_shift.reshape(dt_bias.shape),
        grad_alog.reshape(a_log.shape),
        grad_skip.reshape(d_skip.shape),
        grad_gate.reshape(gate_gain.shape),
        grad_w_out,
    )


def solution(mesh):
    return jax.shard_map(
        per_device,
        mesh=mesh,
        in_specs=(
            P("dp", None),
            P("dp", "row"),
            P("dp", None),
            P("row"),
            P("row", "col"),
            P("row", "col"),
            P("row", "col"),
            P("row", "col"),
            P(None, "col", "row"),
            P("col", "row"),
            P(),
            P(),
            P("col", "row"),
            P("col", "row"),
            P("col", "row"),
            P("col", "row"),
            P("col", "row"),
        ),
        out_specs=(
            P("dp", ("row", "col")),
            P("dp", ("row", "col")),
            P(("row", "col")),
            P("row", "col"),
            P("row", "col"),
            P("row", "col"),
            P("row", "col"),
            P(None, "col", "row"),
            P("col", "row"),
            P(),
            P(),
            P("col", "row"),
            P("col", "row"),
            P("col", "row"),
            P("col", "row"),
            P("col", "row"),
        ),
        check_vma=False,
    )
```

```python
import functools

import jax
import jax.numpy as jnp
from jax import lax
from jax.experimental import pallas as pl
from jax.experimental.pallas import tpu as pltpu
from jax.sharding import PartitionSpec as P

EPS = 1e-05
HIGHEST = lax.Precision.HIGHEST
F32 = jnp.float32
BF16 = jnp.bfloat16
LANES = 128
NEGATIVE = -1e30


def segments(lengths, row_count):
    ends = jnp.cumsum(lengths)
    places = jnp.arange(row_count, dtype=jnp.int32)
    segment = jnp.sum((places[:, None] >= ends[None, :]).astype(jnp.int32), axis=1)
    living = (segment < lengths.shape[0]).astype(F32)
    return (segment, living)


def depthwise(signal, weights, offset_bias, segment):
    row_count = signal.shape[0]
    total = offset_bias[None, :] + weights[0][None, :] * signal
    for offset in range(1, weights.shape[0]):
        moved = jnp.concatenate(
            [jnp.zeros((offset, signal.shape[1]), F32), signal[: row_count - offset]],
            axis=0,
        )
        earlier = jnp.concatenate(
            [jnp.full((offset,), -1, jnp.int32), segment[: row_count - offset]]
        )
        same_seq = (earlier == segment).astype(F32)
        total = total + weights[offset][None, :] * moved * same_seq[:, None]
    return total


def halves(a):
    high = a.astype(BF16)
    return high, (a - high.astype(F32)).astype(BF16)


def dot3(a, b, ca=1, cb=0):
    dims = (((ca,), (cb,)), ((), ()))
    ah, al = halves(a)
    bh, bl = halves(b)

    def one(u, v):
        return lax.dot_general(u, v, dims, preferred_element_type=F32)

    return one(ah, bh) + (one(ah, bl) + one(al, bh))


def dot6(a, b):
    return jnp.dot(a, b, precision=HIGHEST, preferred_element_type=F32)


def iota(shape, axis):
    return lax.broadcasted_iota(jnp.int32, shape, axis)


def decays_of(dt, dt_t, rate_row, rate_col, heads, width):
    rows = dt.shape[0]
    lower = (iota((rows, rows), 0) >= iota((rows, rows), 1)).astype(F32)
    upper = (iota((rows, rows), 0) <= iota((rows, rows), 1)).astype(F32)
    logs = dot6(lower, -dt * rate_row)
    logs_t = dot6(-dt_t * rate_col, upper)
    spread = (iota((heads, width), 0) == iota((heads, width), 1) // (width // heads)).astype(F32)
    return logs, logs_t, upper, spread


def scan_forward(x_ref, b_ref, c_ref, dt_ref, dtt_ref, sc_ref, sr_ref, aux_ref, rr_ref, rc_ref,
                 y_ref, st_ref, state):
    @pl.when(pl.program_id(0) == 0)
    def _():
        state[...] = jnp.zeros_like(state)

    st_ref[0] = state[...]
    rows, width = x_ref.shape
    heads = dt_ref.shape[1]
    each = width // heads
    x, b, c, dt = x_ref[...], b_ref[...], c_ref[...], dt_ref[...]
    logs, logs_t, upper, spread = decays_of(dt, dtt_ref[...], rr_ref[...], rc_ref[...], heads, width)
    keep, last = aux_ref[:, 0:1], aux_ref[:, 1:2]
    grown = dot6(jnp.exp(logs), spread)
    closing = dot6(jnp.exp(logs[rows - 1 :] - logs), spread) * last
    xw = x * dot6(dt, spread)
    before = state[...]
    carried = dot3(c, before) * (grown * keep)
    mask = jnp.logical_and(sc_ref[...] == sr_ref[...], iota((rows, rows), 0) >= iota((rows, rows), 1))
    scores = dot3(c, b, 1, 1)
    per = LANES // each
    lane = iota((rows, LANES), 1) // each
    for group in range(width // LANES):
        cols = slice(group * LANES, (group + 1) * LANES)
        total = carried[:, cols]
        for j in range(per):
            h = group * per + j
            gap = logs[:, h : h + 1] - logs_t[h : h + 1, :]
            weight = jnp.exp(jnp.where(mask, gap, NEGATIVE)) * scores
            total = total + dot3(weight, jnp.where(lane == j, xw[:, cols], 0.0))
        y_ref[:, cols] = total
    held = grown[rows - 1 :] * keep[rows - 1 :]
    state[...] = before * held + dot3(b, xw * closing, 0, 0)


def scan_backward(x_ref, b_ref, c_ref, dt_ref, dtt_ref, sc_ref, sr_ref, aux_ref, rr_ref, rc_ref,
                  y_ref, st_ref, dy_ref, dx_ref, db_ref, dc_ref, ddt_ref, da_ref, dstate):
    @pl.when(pl.program_id(0) == 0)
    def _():
        dstate[...] = jnp.zeros_like(dstate)
        da_ref[...] = jnp.zeros_like(da_ref)

    rows, width = x_ref.shape
    heads = dt_ref.shape[1]
    each = width // heads
    x, b, c, dt, dy = x_ref[...], b_ref[...], c_ref[...], dt_ref[...], dy_ref[...]
    logs, logs_t, upper, spread = decays_of(dt, dtt_ref[...], rr_ref[...], rc_ref[...], heads, width)
    keep, last = aux_ref[:, 0:1], aux_ref[:, 1:2]
    grown = dot6(jnp.exp(logs), spread)
    closing = dot6(jnp.exp(logs[rows - 1 :] - logs), spread) * last
    dt_wide = dot6(dt, spread)
    xw = x * dt_wide
    before, after = st_ref[0], dstate[...]
    held = grown[rows - 1 :] * keep[rows - 1 :]
    u = dy * (grown * keep)
    dc = dot3(u, before, 1, 1)
    v = dot3(b, after)
    xc = xw * closing
    db = dot3(xc, after, 1, 1)
    tail = jnp.sum(before * after, axis=0, keepdims=True) * held + jnp.sum(v * xc, axis=0, keepdims=True)
    dstate[...] = dot3(c, u, 0, 0) + after * held
    mask = jnp.logical_and(sc_ref[...] == sr_ref[...], iota((rows, rows), 0) <= iota((rows, rows), 1))
    scores = dot3(b, c, 1, 1)
    per = LANES // each
    lane = iota((rows, LANES), 1) // each
    dscores = jnp.zeros((rows, rows), F32)
    pieces = []
    for group in range(width // LANES):
        cols = slice(group * LANES, (group + 1) * LANES)
        total = v[:, cols] * closing[:, cols]
        for j in range(per):
            h = group * per + j
            gap = logs_t[h : h + 1, :] - logs[:, h : h + 1]
            decay = jnp.exp(jnp.where(mask, gap, NEGATIVE))
            dyj = jnp.where(lane == j, dy[:, cols], 0.0)
            total = total + dot3(decay * scores, dyj)
            dscores = dscores + dot3(xw[:, cols], dyj, 1, 1) * decay
        pieces.append(total)
    dxw = jnp.concatenate(pieces, axis=1)
    db_ref[...] = db + dot3(dscores, c)
    dc_ref[...] = dc + dot3(dscores, b, 0, 0)
    gather = (iota((width, heads), 0) // each == iota((width, heads), 1)).astype(F32)
    wide = dy * y_ref[...] - xw * dxw
    wide = wide + jnp.where(iota((rows, width), 0) == rows - 1, tail, 0.0)
    dneg = dot6(upper, dot6(wide, gather))
    ddt_ref[...] = dot6(dxw * x, gather) - dneg * rr_ref[...]
    da_ref[...] = da_ref[...] - jnp.sum(dt * dneg, axis=0, keepdims=True)
    dx_ref[...] = dxw * dt_wide


def scan_specs(rows, width, state, heads, count, backward):
    def at(i):
        return count - 1 - i if backward else i

    tall = lambda n: pl.BlockSpec((rows, n), lambda i: (at(i), 0))
    flat = lambda n: pl.BlockSpec((n, rows), lambda i: (0, at(i)))
    fixed = lambda a, b: pl.BlockSpec((a, b), lambda i: (0, 0))
    ins = [tall(width), tall(state), tall(state), tall(heads), flat(heads), tall(1), flat(1),
           tall(2), fixed(1, heads), fixed(heads, 1)]
    states = pl.BlockSpec((1, state, width), lambda i: (at(i), 0, 0))
    return ins, tall, fixed, states


def scan_operands(x, b, c, dt, rates, segment, block):
    row_count = x.shape[0]
    series = segment.reshape(row_count // block, block)
    closing = series[:, -1:]
    previous = jnp.concatenate([jnp.full((1, 1), -1, jnp.int32), closing[:-1]], axis=0)
    aux = jnp.stack(
        [(series == previous).astype(F32).reshape(-1), (series == closing).astype(F32).reshape(-1)],
        axis=1,
    )
    return (x, b, c, dt, dt.T, segment[:, None], segment[None, :], aux, rates[None, :], rates[:, None])


@functools.partial(jax.custom_vjp, nondiff_argnums=(6,))
def state_scan(x, b, c, dt, rates, segment, block):
    return scan_fwd(x, b, c, dt, rates, segment, block)[0]


def scan_fwd(x, b, c, dt, rates, segment, block):
    row_count, width = x.shape
    state, heads = b.shape[1], dt.shape[1]
    count = row_count // block
    ins, tall, fixed, states = scan_specs(block, width, state, heads, count, False)
    y, kept = pl.pallas_call(
        scan_forward,
        grid=(count,),
        in_specs=ins,
        out_specs=[tall(width), states],
        out_shape=[
            jax.ShapeDtypeStruct((row_count, width), F32),
            jax.ShapeDtypeStruct((count, state, width), F32),
        ],
        scratch_shapes=[pltpu.VMEM((state, width), F32)],
        compiler_params=pltpu.CompilerParams(vmem_limit_bytes=48 * 1024 * 1024),
        cost_estimate=pl.CostEstimate(flops=2_000_000_000, bytes_accessed=6_000_000, transcendentals=0),
        name="scan_forward",
    )(*scan_operands(x, b, c, dt, rates, segment, block))
    return y, (x, b, c, dt, rates, segment, y, kept)


def scan_bwd(block, saved, dy):
    x, b, c, dt, rates, segment, y, kept = saved
    row_count, width = x.shape
    state, heads = b.shape[1], dt.shape[1]
    count = row_count // block
    ins, tall, fixed, states = scan_specs(block, width, state, heads, count, True)
    dx, db, dc, ddt, da = pl.pallas_call(
        scan_backward,
        grid=(count,),
        in_specs=ins + [tall(width), states, tall(width)],
        out_specs=[tall(width), tall(state), tall(state), tall(heads), fixed(1, heads)],
        out_shape=[
            jax.ShapeDtypeStruct((row_count, width), F32),
            jax.ShapeDtypeStruct((row_count, state), F32),
            jax.ShapeDtypeStruct((row_count, state), F32),
            jax.ShapeDtypeStruct((row_count, heads), F32),
            jax.ShapeDtypeStruct((1, heads), F32),
        ],
        scratch_shapes=[pltpu.VMEM((state, width), F32)],
        compiler_params=pltpu.CompilerParams(vmem_limit_bytes=48 * 1024 * 1024),
        cost_estimate=pl.CostEstimate(flops=6_000_000_000, bytes_accessed=10_000_000, transcendentals=0),
        name="scan_backward",
    )(*scan_operands(x, b, c, dt, rates, segment, block), y, kept, dy)
    return dx, db, dc, ddt, da[0], None


state_scan.defvjp(scan_fwd, scan_bwd)


def mixer(x_part, bc_part, z_part, dt_part, conv_w, conv_b, bc_w, bc_b, dt_shift, a_logs, skips,
          segment, living):
    row_count, width = x_part.shape
    heads = dt_shift.shape[0]
    x_act = jax.nn.silu(depthwise(x_part, conv_w, conv_b, segment))
    bc_act = jax.nn.silu(depthwise(bc_part, bc_w, bc_b, segment))
    state = bc_act.shape[1] // 2
    steps = jax.nn.softplus(dt_part + dt_shift[None, :])
    block = min(row_count, 256)
    scanned = state_scan(
        x_act, bc_act[:, :state], bc_act[:, state:], steps, jnp.exp(a_logs), segment, block
    )
    scanned = scanned + jnp.repeat(skips, width // heads)[None, :] * x_act
    return scanned * jax.nn.silu(z_part) * living[:, None]


def swap(value, axis):
    count = lax.axis_size(axis)
    return lax.ppermute(value, axis, [(i, (i + 1) % count) for i in range(count)])


def part(value, index, axis):
    size = value.shape[axis] // 2
    return lax.dynamic_slice_in_dim(value, index * size, size, axis)


def ordered(own, other, index, axis):
    first = index == 0
    return jnp.concatenate([jnp.where(first, own, other), jnp.where(first, other, own)], axis=axis)


def dot(a, b):
    return jnp.dot(a, b, preferred_element_type=F32)


def per_device(hidden, out_grad, seq_lens, rmsnorm_gain, w_z, w_x, w_bc, w_dt, conv_x, conv_x_bias,
               conv_bc, conv_bc_bias, dt_bias, a_log, d_skip, gate_gain, w_out):
    row_count, model_width = hidden.shape
    row, col = lax.axis_index("row"), lax.axis_index("col")
    batches = lax.axis_size("dp")
    shares = lax.axis_size("row") * lax.axis_size("col")
    inner_width = w_z.shape[1] * lax.axis_size("col")
    half = model_width // 2

    def own_heads(weight, axis):
        mine = part(weight, row, axis)
        theirs = swap(part(weight, 1 - row, axis), "row")
        return jnp.concatenate([mine, theirs], axis=1 - axis)

    wx = own_heads(w_x, 1)
    wbc_rows = jnp.concatenate([w_bc, swap(w_bc, "row")], axis=0)
    wbc = ordered(wbc_rows, swap(wbc_rows, "col"), col, 1)
    wdt = own_heads(w_dt, 1)
    gain = jnp.concatenate([rmsnorm_gain, swap(rmsnorm_gain, "row")])
    wx, wbc_rows, w_z, w_out, out_grad = lax.optimization_barrier(
        (wx, wbc_rows, w_z, w_out, out_grad)
    )
    wz = own_heads(w_z, 1)
    incoming = jnp.concatenate([out_grad, swap(out_grad, "row")], axis=1)
    wo = own_heads(w_out, 0)

    segment, living = segments(seq_lens[0], row_count)
    whole = hidden.astype(F32)
    whole = jnp.where(row == 0, whole, jnp.concatenate([whole[:, half:], whole[:, :half]], axis=1))
    scale = lax.rsqrt(jnp.mean(whole * whole, axis=1) + EPS)
    xhat = whole * scale[:, None]
    normed = (xhat * gain[None, :]).astype(BF16)
    x_in = dot(normed, wx)
    bc_in = dot(normed, wbc)
    dt_in = dot(normed, wdt)
    z_in = dot(normed, wz)
    gain_flat = gate_gain.reshape(-1)

    def local_mix(*parts):
        return mixer(*parts, segment, living)

    mixed, pull = jax.vjp(
        local_mix, x_in, bc_in, z_in, dt_in, conv_x.reshape(conv_x.shape[0], -1),
        conv_x_bias.reshape(-1), conv_bc, conv_bc_bias, dt_bias.reshape(-1), a_log.reshape(-1),
        d_skip.reshape(-1),
    )
    d_gated = dot(incoming, wo.T)
    sums = jnp.stack(
        [jnp.sum(mixed * mixed, axis=1), jnp.sum(mixed * gain_flat[None, :] * d_gated, axis=1)]
    )
    sums = lax.psum(sums, ("row", "col"))
    inv_gate = lax.rsqrt(sums[0] / inner_width + EPS)
    inner = sums[1]
    gated = (mixed * inv_gate[:, None] * gain_flat[None, :]).astype(BF16)
    d_mixed = (
        inv_gate[:, None] * gain_flat[None, :] * d_gated
        - mixed * (inv_gate**3 / inner_width)[:, None] * inner[:, None]
    )

    def scattered(partial):
        kept = partial[:, :half] + swap(partial[:, half:].astype(BF16), "row").astype(F32)
        return part(kept, col, 1) + swap(part(kept, 1 - col, 1).astype(BF16), "col").astype(F32)

    grad_wo = dot(gated.T, incoming).astype(BF16)
    wo_piece = lax.psum_scatter(grad_wo, "dp", scatter_dimension=0, tiled=True)
    wo_pair = jnp.stack([wo_piece[:, :half], swap(wo_piece[:, half:], "row")])
    wo_pair = jnp.where(row == 0, wo_pair, wo_pair[::-1])
    wo_all = lax.all_gather(wo_pair, "dp", axis=1, tiled=True)
    grad_w_out = wo_all.reshape(-1, half).astype(F32)

    out_sum = scattered(dot(gated, wo))
    block_out = (part(whole[:, :half], col, 1) + out_sum).astype(BF16)
    grad_gate = jnp.sum(d_gated * mixed * inv_gate[:, None], axis=0)

    (grad_x, grad_bc, grad_z, grad_dt, grad_cw, grad_cb, grad_bw, grad_bb, grad_shift, grad_alog,
     grad_skip) = pull(d_mixed)
    dz, dx, ddt, dbc = (v.astype(BF16) for v in (grad_z, grad_x, grad_dt, grad_bc))

    steps = ddt.shape[1]
    grads = jnp.concatenate(
        [dz, dx, dbc, ddt, jnp.zeros((row_count, LANES - steps), BF16)], axis=1
    )
    big = dot(normed.T, grads).astype(BF16)
    wide = big.shape[1]
    big = big.reshape(2, batches, -1, wide).transpose(1, 0, 2, 3).reshape(-1, wide)
    piece = lax.psum_scatter(big, "dp", scatter_dimension=0, tiled=True)
    back = dot(dz, wz.T) + dot(dx, wx.T) + dot(ddt, wdt.T) + dot(dbc, wbc.T)
    d_normed = scattered(back)
    xhat_own = part(xhat[:, :half], col, 1)
    scaled = d_normed * part(rmsnorm_gain, col, 0)[None, :]
    total = lax.psum(jnp.sum(scaled * xhat_own, axis=1), ("row", "col"))
    hidden_input_gradient = (
        part(out_grad, col, 1).astype(F32)
        + scale[:, None] * (scaled - xhat_own * (total / model_width)[:, None])
    ).astype(BF16)
    norm_gradient = jnp.sum(d_normed * xhat_own, axis=0)

    small = (grad_bw, grad_bb, norm_gradient, grad_cw, grad_cb, grad_shift, grad_alog, grad_skip,
             grad_gate)
    shared = jnp.concatenate([grad_bw.reshape(-1), grad_bb])
    shared = shared + swap(shared, "row")
    shared = shared + swap(shared, "col")
    packed = jnp.concatenate([shared] + [v.reshape(-1) for v in small[2:]])
    distance = 1
    while distance < batches:
        packed = packed + lax.ppermute(packed, "dp", [(i, i ^ distance) for i in range(batches)])
        distance *= 2
    sums, start = [], 0
    for v in small:
        sums.append(packed[start : start + v.size].reshape(v.shape))
        start += v.size
    (grad_bw, grad_bb, norm_gradient, grad_cw, grad_cb, grad_shift, grad_alog, grad_skip,
     grad_gate) = sums
    piece, packed, hidden_input_gradient = lax.optimization_barrier(
        (piece, packed, hidden_input_gradient)
    )
    piece = piece.reshape(2, -1, wide)
    mine, theirs = piece[0], swap(piece[1], "row")
    nz, nbc = dz.shape[1], dbc.shape[1]
    bc_sum = (mine[:, 2 * nz : 2 * nz + nbc].astype(F32)
              + theirs[:, 2 * nz : 2 * nz + nbc].astype(F32))
    bc_sum = part(bc_sum, col, 1) + swap(part(bc_sum, 1 - col, 1).astype(BF16), "col").astype(F32)
    pieces = jnp.concatenate(
        [
            ordered(mine[:, :nz], theirs[:, :nz], row, 1),
            ordered(mine[:, nz : 2 * nz], theirs[:, nz : 2 * nz], row, 1),
            bc_sum.astype(BF16),
            jnp.where(row == 0, mine[:, 2 * nz + nbc :], theirs[:, 2 * nz + nbc :]),
            jnp.where(row == 0, theirs[:, 2 * nz + nbc :], mine[:, 2 * nz + nbc :]),
        ],
        axis=1,
    )
    whole_grads = lax.all_gather(pieces, "dp", axis=0, tiled=True)
    grad_wz = whole_grads[:, : 2 * nz].astype(F32)
    grad_wx = whole_grads[:, 2 * nz : 4 * nz].astype(F32)
    at = 4 * nz
    grad_wbc = whole_grads[:, at : at + nbc // 2].astype(F32)
    at = at + nbc // 2
    grad_wdt = jnp.concatenate(
        [whole_grads[:, at : at + steps], whole_grads[:, at + LANES : at + LANES + steps]], axis=1
    ).astype(F32)

    return (
        block_out,
        hidden_input_gradient,
        norm_gradient,
        grad_wz,
        grad_wx,
        grad_wbc,
        grad_wdt,
        grad_cw.reshape(conv_x.shape),
        grad_cb.reshape(conv_x_bias.shape),
        grad_bw,
        grad_bb,
        grad_shift.reshape(dt_bias.shape),
        grad_alog.reshape(a_log.shape),
        grad_skip.reshape(d_skip.shape),
        grad_gate.reshape(gate_gain.shape),
        grad_w_out,
    )


def solution(mesh):
    return jax.shard_map(
        per_device,
        mesh=mesh,
        in_specs=(
            P("dp", None),
            P("dp", "row"),
            P("dp", None),
            P("row"),
            P("row", "col"),
            P("row", "col"),
            P("row", "col"),
            P("row", "col"),
            P(None, "col", "row"),
            P("col", "row"),
            P(),
            P(),
            P("col", "row"),
            P("col", "row"),
            P("col", "row"),
            P("col", "row"),
            P("col", "row"),
        ),
        out_specs=(
            P("dp", ("row", "col")),
            P("dp", ("row", "col")),
            P(("row", "col")),
            P("row", "col"),
            P("row", "col"),
            P("row", "col"),
            P("row", "col"),
            P(None, "col", "row"),
            P("col", "row"),
            P(),
            P(),
            P("col", "row"),
            P("col", "row"),
            P("col", "row"),
            P("col", "row"),
            P("col", "row"),
        ),
        check_vma=False,
    )
```
